32 devices in a mesh: lev: 4 (over y, x), wave: 8 (over z, core).
Axes of the slice: x: 2, y: 2, z: 4, core: 2. Of those that a mesh axis runs over, the one named last changes fastest.
Arguments:
- vorticity: float32 [2, 32, 640, 640], P(None, 'lev', 'wave'), may hold values from -6 to 6
- wind_lam: float32 [32, 640, 1280], P('lev', 'wave'), may hold values from -6 to 6
- wind_mu: float32 [32, 640, 1280], P('lev', 'wave'), may hold values from -6 to 6
- modes: float32 [32, 32], replicated, may hold values from -0.5 to 1.5, as said below
- mode_rates: float32 [32], replicated, may hold values from 0.05 to 2
- wave_order: int32 [640], replicated, may hold values from 0 to 639, each once
- lat_order: int32 [640], replicated, may hold values from 0 to 639, each once
Outputs:
- advanced: float32 [2, 32, 640, 640], P(None, 'lev', 'wave')
- stream: float32 [2, 32, 640, 640], P(None, 'lev', 'wave')
The draws below stay inside these ranges and needn't reach their ends.
Inputs may be any that keep to these rules, and one draw needn't show every extreme that they name: `wave_order`: A permutation: each wavenumber 0 to 639 is held by exactly one slot. `lat_order`: A permutation: each latitude 0 to 639 is held by exactly one slot. `modes`: A dense real matrix.
All inputs are finite; a program needn't handle non-finite values.
Results may differ from the reference program's by a relative error of at most 0.0003.
Values sent between devices are 32-bit elements; how exact they have to be, the bound alone decides.
A program may use at most 320 MiB of HBM per device.

```python
import math
import jax
import jax.numpy as jnp
from jax import lax

M = 640
LAT = 640
GRID_LONGITUDES = 1280
LEV = 32


def draw_modes(key, part):
    noise = jax.random.truncated_normal(key, -2.5, 2.5, (LEV, LEV), jnp.float32)
    return jnp.eye(LEV, dtype=jnp.float32) + 0.6 / math.sqrt(LEV) * noise


def levels(own_key, dims, split, least, top_value):
    gain, own = 1.0, jax.random.fold_in(own_key, 6)
    for position, shards_of in split:
        steps = jnp.exp(jax.random.uniform(jax.random.fold_in(own, position), (shards_of,), jnp.float32, least / len(split), top_value / len(split)))
        gain = gain * jnp.repeat(steps, dims[position] // shards_of).reshape([-1 if axis == position else 1 for axis in range(len(dims))])
    return gain


def bell_draw(rng, shape, spread, most, cuts=(), kind=jnp.bfloat16):
    level = levels(rng, shape, cuts, -0.22, 0.18) if cuts else 1.0
    entries = jax.random.normal(rng, shape, jnp.float32) * spread * level
    return jnp.minimum(jnp.maximum(entries, -most), most).astype(kind)


def setup_inputs(seed: int = 0) -> dict:
    seeds = jax.random.split(jax.random.key(seed), 8)
    vorticity = bell_draw(seeds[0], (2, LEV, M, M), 1.0, 6.0, ((1, 4), (2, 8)), jnp.float32)
    wind_lam = bell_draw(seeds[1], (LEV, LAT, GRID_LONGITUDES), 1.0, 6.0, ((0, 4), (1, 8)), jnp.float32)
    wind_mu = bell_draw(seeds[2], (LEV, LAT, GRID_LONGITUDES), 1.0, 6.0, ((0, 4), (1, 8)), jnp.float32)
    modes = draw_modes(jax.random.fold_in(seeds[7], 71), 0)
    mode_rates = jnp.clip(jnp.exp(jax.random.uniform(seeds[4], (LEV,), jnp.float32, math.log(0.05), math.log(2.0))), 0.05, 2.0)
    wave_order = jax.random.permutation(seeds[5], M).astype(jnp.int32)
    lat_order = jax.random.permutation(seeds[6], LAT).astype(jnp.int32)
    return {"vorticity": vorticity, "wind_lam": wind_lam, "wind_mu": wind_mu, "modes": modes, "mode_rates": mode_rates, "wave_order": wave_order, "lat_order": lat_order}


HIGH_ACCURACY = lax.Precision.HIGHEST
TIME_STEP = 0.4

def latitudes(lat_order):
    angles = math.pi * (lat_order.astype(jnp.float32) + 0.75) / (LAT + 0.5)
    sines = jnp.sin(angles)
    return (jnp.cos(angles), sines, math.pi / (LAT + 0.5) * sines)

def legendre(waves, cosines, sines, degrees):
    wavenum = waves.astype(jnp.float32)[:, None]
    counter = jnp.arange(1, M, dtype=jnp.int32).astype(jnp.float32)
    halves = 0.5 * jnp.log((2.0 * counter + 1.0) / (2.0 * counter))
    start_log = lax.optimization_barrier(jnp.sum(jnp.where(counter[None, :] <= wavenum, halves[None, :], 0.0), axis=1))
    log_start = -0.5 * math.log(2.0) + start_log[:, None] + wavenum * jnp.log(sines)[None, :]

    def advance(carry, step_index):
        previous, current, log_scale = carry
        emitted = current * jnp.exp(log_scale)
        degree = wavenum + step_index.astype(jnp.float32) + 1.0
        factor_ahead = jnp.sqrt((4.0 * degree * degree - 1.0) / (degree * degree - wavenum * wavenum))
        lower_degree = degree - 1.0
        factor_behind = jnp.sqrt((lower_degree * lower_degree - wavenum * wavenum) / (4.0 * lower_degree * lower_degree - 1.0))
        following = factor_ahead * (cosines[None, :] * current - factor_behind * previous)
        magnitude = jnp.abs(current) + jnp.abs(following)
        return ((current / magnitude, following / magnitude, log_scale + jnp.log(magnitude)), emitted)
    initial = (jnp.zeros(log_start.shape, jnp.float32), jnp.ones(log_start.shape, jnp.float32), log_start)
    last_carry, stacked = lax.scan(advance, initial, jnp.arange(degrees, dtype=jnp.int32), unroll=32)
    live_mask = (waves[:, None] + jnp.arange(degrees, dtype=jnp.int32)[None, :] < M).astype(jnp.float32)
    return jnp.transpose(stacked, (1, 0, 2)) * live_mask[:, :, None]

def coupling(waves):
    wavenum = waves.astype(jnp.float32)[:, None]
    degree = wavenum + jnp.arange(M, dtype=jnp.int32).astype(jnp.float32)[None, :]
    live_mask = (degree < M - 0.5).astype(jnp.float32)
    square = wavenum * wavenum
    eps_here = jnp.sqrt((degree * degree - square) / (4.0 * degree * degree - 1.0))
    degree_next = degree + 1.0
    eps_ahead = jnp.sqrt((degree_next * degree_next - square) / (4.0 * degree_next * degree_next - 1.0))
    kappa = degree * (degree + 1.0) / (M * (M + 1.0))
    return (-(degree - 1.0) * eps_here * live_mask, (degree + 2.0) * eps_ahead * live_mask, live_mask, kappa)

def fourier(waves):
    phase = waves[:, None] * jnp.arange(GRID_LONGITUDES, dtype=jnp.int32)[None, :] % GRID_LONGITUDES
    angles = 2.0 * math.pi / GRID_LONGITUDES * phase.astype(jnp.float32)
    return jnp.concatenate([jnp.cos(angles), jnp.sin(angles)], axis=0)

def lowered(spectra):
    return jnp.concatenate([jnp.zeros_like(spectra[..., :1]), spectra[..., :-1]], axis=-1)

def raised(spectra):
    return jnp.concatenate([spectra[..., 1:], jnp.zeros_like(spectra[..., :1])], axis=-1)

def tendency(spectra, waves, cosines, sines, weights, wind_lam, wind_mu, lower, upper, group):
    meridional = lower * lowered(spectra) + upper * raised(spectra)
    both = jnp.stack([spectra, meridional])
    count = M // group

    def inverse_block(index):
        first = index * group
        block_table = legendre(lax.dynamic_slice_in_dim(waves, first, group), cosines, sines, M)
        block_fields = lax.dynamic_slice_in_dim(both, first, group, 3)
        return jnp.einsum('fclsj,sjr->fclsr', block_fields, block_table, precision=HIGH_ACCURACY)
    pieces = lax.map(inverse_block, jnp.arange(count, dtype=jnp.int32))
    at_lat = jnp.moveaxis(pieces, 0, 3).reshape(2, 2, LEV, M, LAT)
    double = jnp.where(waves == 0, 1.0, 2.0).astype(jnp.float32)
    scaled = double * waves.astype(jnp.float32)
    zonal = jnp.concatenate([-(scaled[:, None] * at_lat[0, 1]), -(scaled[:, None] * at_lat[0, 0])], axis=1)
    merid = jnp.concatenate([double[:, None] * at_lat[1, 0], -(double[:, None] * at_lat[1, 1])], axis=1)
    trigonometric_table = fourier(waves)
    grid = jnp.einsum('flsr,sk->flrk', jnp.stack([zonal, merid]), trigonometric_table, precision=HIGH_ACCURACY)
    source_term = -(wind_lam * grid[0] + wind_mu * grid[1])
    spectral_latitude_fields = jnp.einsum('nqy,zy->nzq', source_term, trigonometric_table, precision=HIGH_ACCURACY) / GRID_LONGITUDES
    returned = jnp.stack([spectral_latitude_fields[:, :M], -spectral_latitude_fields[:, M:]]) * weights

    def forward_block(index):
        first = index * group
        block_table = legendre(lax.dynamic_slice_in_dim(waves, first, group), cosines, sines, M)
        block_fields = lax.dynamic_slice_in_dim(returned, first, group, 2)
        return jnp.einsum('clsr,sjr->clsj', block_fields, block_table, precision=HIGH_ACCURACY)
    pieces = lax.map(forward_block, jnp.arange(count, dtype=jnp.int32))
    return jnp.moveaxis(pieces, 0, 2).reshape(2, LEV, M, M)

def reference(vorticity, wind_lam, wind_mu, modes, mode_rates, wave_order, lat_order):
    cosines, sines, weights = latitudes(lat_order)
    lower, upper, live_mask, kappa = coupling(wave_order)
    group = math.gcd(M, 64)
    start = vorticity * live_mask
    first_rate = tendency(start, wave_order, cosines, sines, weights, wind_lam, wind_mu, lower, upper, group)
    middle = start + TIME_STEP / M * first_rate
    second_rate = tendency(middle, wave_order, cosines, sines, weights, wind_lam, wind_mu, lower, upper, group)
    advanced = start + 0.5 * TIME_STEP / M * (first_rate + second_rate)
    projected = jnp.einsum('lk,clsj->cksj', modes, advanced, precision=HIGH_ACCURACY)
    projected = projected / (kappa[None, None] + mode_rates[None, :, None, None])
    stream = jnp.einsum('lk,cksj->clsj', modes, projected, precision=HIGH_ACCURACY) * live_mask
    return (advanced, stream)
```

```python
import functools
import math

import jax
import jax.numpy as jnp
from jax import lax
from jax.experimental import pallas as pl
from jax.experimental.pallas import tpu as pltpu
from jax.sharding import PartitionSpec as P

M = 640
LAT = 640
GRID_LONGITUDES = 1280


HIGH_ACCURACY = lax.Precision.HIGH
TIME_STEP = 0.4


def latitudes(lat_order):
    angles = math.pi * (lat_order.astype(jnp.float32) + 0.75) / (LAT + 0.5)
    sines = jnp.sin(angles)
    return (jnp.cos(angles), sines, math.pi / (LAT + 0.5) * sines)


GROUP = 8
LANES = 128
VMEM = 60 * 1024 * 1024


def table_kernel(ahead_ref, behind_ref, start_ref, cos_ref, out_ref):
    lats = out_ref.shape[2]
    spans = [(k, min(LANES, lats - k)) for k in range(0, lats, LANES)]
    mus = [jnp.broadcast_to(cos_ref[0:1, k : k + n], (GROUP, n)) for k, n in spans]

    def block(index, carry):
        first = pl.multiple_of(index * 8, 8)
        ahead = [ahead_ref[first + t] for t in range(8)]
        behind = [behind_ref[first + t] for t in range(8)]
        following_carry = []
        for (k, n), mu, (previous, current, log_scale) in zip(spans, mus, carry):
            scale = jnp.exp(log_scale)
            rows = []
            for t in range(8):
                rows.append(current * scale)
                following = ahead[t][:, :n] * (mu * current - behind[t][:, :n] * previous)
                previous, current = current, following
            magnitude = jnp.abs(previous) + jnp.abs(current)
            following_carry.append(
                (previous / magnitude, current / magnitude, log_scale + jnp.log(magnitude))
            )
            out_ref[:, pl.ds(first, 8), k : k + n] = jnp.swapaxes(jnp.stack(rows), 0, 1)
        return tuple(following_carry)

    initial = tuple(
        (
            jnp.zeros((GROUP, n), jnp.float32),
            jnp.ones((GROUP, n), jnp.float32),
            start_ref[:, k : k + n],
        )
        for k, n in spans
    )
    lax.fori_loop(0, out_ref.shape[1] // 8, block, initial)


def legendre(waves, cosines, sines, degrees):
    wavenum = waves.astype(jnp.float32)[:, None]
    counter = jnp.arange(1, M, dtype=jnp.int32).astype(jnp.float32)
    halves = 0.5 * jnp.log((2.0 * counter + 1.0) / (2.0 * counter))
    start_log = jnp.sum(jnp.where(counter[None, :] <= wavenum, halves[None, :], 0.0), axis=1)
    log_start = -0.5 * math.log(2.0) + start_log[:, None] + wavenum * jnp.log(sines)[None, :]
    degree = wavenum.T + jnp.arange(degrees, dtype=jnp.int32).astype(jnp.float32)[:, None] + 1.0
    square = wavenum.T * wavenum.T
    ahead = jnp.sqrt((4.0 * degree * degree - 1.0) / (degree * degree - square))
    lower = degree - 1.0
    behind = jnp.sqrt((lower * lower - square) / (4.0 * lower * lower - 1.0))
    slots, lats = waves.shape[0], cosines.shape[0]
    wide = (degrees, slots, LANES)
    coefficient = pl.BlockSpec((degrees, GROUP, LANES), lambda g: (0, g, 0))
    return pl.pallas_call(
        table_kernel,
        grid=(slots // GROUP,),
        in_specs=[
            coefficient,
            coefficient,
            pl.BlockSpec((GROUP, lats), lambda g: (g, 0)),
            pl.BlockSpec((1, lats), lambda g: (0, 0)),
        ],
        out_specs=pl.BlockSpec((GROUP, degrees, lats), lambda g: (g, 0, 0)),
        out_shape=jax.ShapeDtypeStruct((slots, degrees, lats), jnp.float32),
        compiler_params=pltpu.CompilerParams(vmem_limit_bytes=VMEM),
        name="table",
    )(
        jnp.broadcast_to(ahead[:, :, None], wide),
        jnp.broadcast_to(behind[:, :, None], wide),
        log_start,
        cosines[None, :],
    )


def halves_of(value):
    high = value.astype(jnp.bfloat16)
    return high, (value - high.astype(jnp.float32)).astype(jnp.bfloat16)


def three_products(fields, table, contract):
    rows = fields.shape[0]
    field_high, field_low = halves_of(fields)
    table_high, table_low = halves_of(table)
    dims = (((1,), (contract,)), ((), ()))
    both = lax.dot_general(
        jnp.concatenate([field_high, field_low], axis=0),
        table_high,
        dims,
        preferred_element_type=jnp.float32,
    )
    small = lax.dot_general(field_high, table_low, dims, preferred_element_type=jnp.float32)
    return both[:rows] + (both[rows:] + small)


def transform_kernel(waves_ref, fields_ref, table_ref, out_ref, turned, result, *, forward):
    degrees = table_ref.shape[1]
    turned[...] = jnp.swapaxes(fields_ref[...], 0, 1)
    group = pl.program_id(0)
    for i in range(GROUP):
        alive = degrees - waves_ref[group * GROUP + i]
        for first in range(0, degrees, 256):
            last = min(first + 256, degrees)

            @pl.when(alive > first)
            def _():
                table = table_ref[i, first:last, :]
                if forward:
                    result[i, :, first:last] = three_products(turned[i], table, 1)
                elif first == 0:
                    result[i] = three_products(turned[i, :, first:last], table, 0)
                else:
                    result[i] += three_products(turned[i, :, first:last], table, 0)

            if forward:

                @pl.when(alive <= first)
                def _():
                    result[i, :, first:last] = jnp.zeros(
                        (result.shape[1], last - first), jnp.float32
                    )

    out_ref[...] = jnp.swapaxes(result[...], 0, 1)


def transform(waves, fields, table, forward):
    rows, slots, width = fields.shape
    degrees, lats = table.shape[1:]
    out_width = degrees if forward else lats
    return pl.pallas_call(
        functools.partial(transform_kernel, forward=forward),
        grid_spec=pltpu.PrefetchScalarGridSpec(
            num_scalar_prefetch=1,
            grid=(slots // GROUP,),
            in_specs=[
                pl.BlockSpec((rows, GROUP, width), lambda g, w: (0, g, 0)),
                pl.BlockSpec((GROUP, degrees, lats), lambda g, w: (g, 0, 0)),
            ],
            out_specs=pl.BlockSpec((rows, GROUP, out_width), lambda g, w: (0, g, 0)),
            scratch_shapes=[
                pltpu.VMEM((GROUP, rows, width), jnp.float32),
                pltpu.VMEM((GROUP, rows, out_width), jnp.float32),
            ],
        ),
        out_shape=jax.ShapeDtypeStruct((rows, slots, out_width), jnp.float32),
        compiler_params=pltpu.CompilerParams(vmem_limit_bytes=VMEM),
        name="analysis" if forward else "synthesis",
    )(waves, fields, table)


def padded(array, axis, size):
    widths = [(0, 0)] * array.ndim
    widths[axis] = (0, size - array.shape[axis])
    return jnp.pad(array, widths) if size > array.shape[axis] else array


def coupling(waves):
    wavenum = waves.astype(jnp.float32)[:, None]
    degree = wavenum + jnp.arange(M, dtype=jnp.int32).astype(jnp.float32)[None, :]
    live_mask = (degree < M - 0.5).astype(jnp.float32)
    square = wavenum * wavenum
    eps_here = jnp.sqrt((degree * degree - square) / (4.0 * degree * degree - 1.0))
    degree_next = degree + 1.0
    eps_ahead = jnp.sqrt(
        (degree_next * degree_next - square) / (4.0 * degree_next * degree_next - 1.0)
    )
    kappa = degree * (degree + 1.0) / (M * (M + 1.0))
    return (
        -(degree - 1.0) * eps_here * live_mask,
        (degree + 2.0) * eps_ahead * live_mask,
        live_mask,
        kappa,
    )


def fourier(waves):
    phase = waves[:, None] * jnp.arange(GRID_LONGITUDES, dtype=jnp.int32)[None, :] % GRID_LONGITUDES
    angles = 2.0 * math.pi / GRID_LONGITUDES * phase.astype(jnp.float32)
    return jnp.concatenate([jnp.cos(angles), jnp.sin(angles)], axis=0)


def lowered(spectra):
    return jnp.concatenate([jnp.zeros_like(spectra[..., :1]), spectra[..., :-1]], axis=-1)


def raised(spectra):
    return jnp.concatenate([spectra[..., 1:], jnp.zeros_like(spectra[..., :1])], axis=-1)


def on_device(vorticity, wind_lam, wind_mu, modes, mode_rates, wave_order, lat_order):
    slots = vorticity.shape[2]
    wave_pos = lax.axis_index("wave")
    lev_pos = lax.axis_index("lev")
    waves = lax.dynamic_slice_in_dim(wave_order, wave_pos * slots, slots)
    cosines, sines, weights = latitudes(lat_order)
    full = -(-slots // GROUP) * GROUP
    full_waves = padded(waves, 0, full)
    legendre_table = legendre(full_waves, cosines, sines, M)
    lower, upper, live_mask, kappa = coupling(waves)
    trigonometric_table = fourier(wave_order)
    double = jnp.where(wave_order == 0, 1.0, 2.0).astype(jnp.float32)
    scaled = double * wave_order.astype(jnp.float32)

    def tendency(spectra):
        meridional = lower * lowered(spectra) + upper * raised(spectra)
        both = jnp.stack([spectra, meridional])
        rows = both.shape[0] * both.shape[1] * both.shape[2]
        flat = padded(both.reshape(rows, slots, M), 1, full)
        at_lat = transform(full_waves, flat, legendre_table, False)[:, :slots]
        at_lat = at_lat.reshape(both.shape[:4] + (LAT,))
        at_lat = lax.all_to_all(at_lat, "wave", split_axis=4, concat_axis=3, tiled=True)
        zonal = jnp.concatenate(
            [-(scaled[:, None] * at_lat[0, 1]), -(scaled[:, None] * at_lat[0, 0])], axis=1
        )
        merid = jnp.concatenate(
            [double[:, None] * at_lat[1, 0], -(double[:, None] * at_lat[1, 1])], axis=1
        )
        grid = jnp.einsum(
            "flsr,sk->flrk", jnp.stack([zonal, merid]), trigonometric_table, precision=HIGH_ACCURACY
        )
        source_term = -(wind_lam * grid[0] + wind_mu * grid[1])
        spectral_latitude_fields = (
            jnp.einsum("nqy,zy->nzq", source_term, trigonometric_table, precision=HIGH_ACCURACY)
            / GRID_LONGITUDES
        )
        returned = jnp.stack([spectral_latitude_fields[:, :M], -spectral_latitude_fields[:, M:]])
        returned = (
            lax.all_to_all(returned, "wave", split_axis=2, concat_axis=3, tiled=True) * weights
        )
        flat = padded(returned.reshape(rows // 2, slots, LAT), 1, full)
        result = transform(full_waves, flat, legendre_table, True)[:, :slots]
        return result.reshape(spectra.shape) * live_mask

    start = vorticity * live_mask
    first_rate = tendency(start)
    middle = start + TIME_STEP / M * first_rate
    second_rate = tendency(middle)
    advanced = start + 0.5 * TIME_STEP / M * (first_rate + second_rate)
    regrouped_fields = lax.all_to_all(advanced, "lev", split_axis=3, concat_axis=1, tiled=True)
    block_width = regrouped_fields.shape[3]
    diffusion_block = lax.dynamic_slice_in_dim(kappa, lev_pos * block_width, block_width, 1)
    projected = jnp.einsum("lk,clsj->cksj", modes, regrouped_fields, precision=HIGH_ACCURACY)
    projected = projected / (diffusion_block[None, None] + mode_rates[None, :, None, None])
    restored = jnp.einsum("lk,cksj->clsj", modes, projected, precision=HIGH_ACCURACY)
    stream = lax.all_to_all(restored, "lev", split_axis=1, concat_axis=3, tiled=True)
    stream = stream * live_mask
    return (advanced, stream)


def solution(mesh):
    placed = (
        P(None, "lev", "wave", None),
        P("lev", "wave", None),
        P("lev", "wave", None),
        P(),
        P(),
        P(),
        P(),
    )
    return jax.shard_map(
        on_device,
        mesh=mesh,
        in_specs=placed,
        out_specs=(P(None, "lev", "wave", None), P(None, "lev", "wave", None)),
        check_vma=False,
    )
```
